512 devices in a mesh: tok: 16 (over z), scol: 4 (over y), tcol: 8 (over x, core).
Axes of the slice: x: 4, y: 4, z: 16, core: 2. Of those that a mesh axis runs over, the one named last changes fastest.
Arguments:
- student: float32 [8192, 4096], P('tok', 'scol'), may hold values from -6 to 6
- teacher: float32 [8192, 4096], P('tok', 'tcol'), may hold values from -6 to 6
- teacher_norm: float32 [1], replicated, may hold values from 262144 to 1048576
Outputs:
- student_grad: float32 [8192, 4096], P(('tok', 'tcol'), 'scol')
The draws below stay inside these ranges and needn't reach their ends.
All inputs are finite; a program needn't handle non-finite values.
Results may differ from the reference program's by a relative error of at most 0.000073.
Values sent between devices are 32-bit elements; how exact they have to be, the bound alone decides.
A program may use at most 64 MiB of HBM per device.

```python
import math
import jax
import jax.numpy as jnp
from jax import lax

DS = 4096
DT = 4096
TOKENS = 8192


def shard_levels(rng, extent, cuts, low, largest):
    loudness = 1.0
    for position, parts in cuts:
        draws = jax.random.uniform(jax.random.fold_in(jax.random.fold_in(rng, 6), position), (parts,), jnp.float32, low / len(cuts), largest / len(cuts))
        loudness = loudness * jnp.repeat(jnp.exp(draws), extent[position] // parts).reshape((-1,) + (1,) * (len(extent) - 1 - position))
    return loudness


def scatter_about(own_key, extent, scale, bound, split=(), dtype=jnp.bfloat16):
    gain = shard_levels(own_key, extent, split, -0.22, 0.18) if split else 1.0
    drawn = jax.random.normal(own_key, extent, jnp.float32) * scale * gain
    return jnp.minimum(jnp.maximum(drawn, -bound), bound).astype(dtype)


def setup_inputs(seed: int = 0) -> dict:
    arg_keys = jax.random.split(jax.random.key(seed), 4)
    student = scatter_about(arg_keys[0], (TOKENS, DS), 1.0, 6.0, ((0, 16), (1, 4)), jnp.float32)
    teacher = scatter_about(arg_keys[1], (TOKENS, DT), 1.0, 6.0, ((0, 16), (1, 8)), jnp.float32)
    teacher_norm = jnp.clip(jnp.exp(jax.random.uniform(arg_keys[2], (1,), jnp.float32, math.log(262144.0), math.log(1048576))), 262144.0, 1048576)
    return {"student": student, "teacher": teacher, "teacher_norm": teacher_norm}


def reference(student, teacher, teacher_norm):
    highest = lax.Precision.HIGHEST
    cross = jnp.dot(student.T, teacher, precision=highest, preferred_element_type=jnp.float32)
    gram = jnp.dot(student.T, student, precision=highest, preferred_element_type=jnp.float32)
    hsic = jnp.sum(cross * cross)
    gram_sq = jnp.sum(gram * gram)
    student_norm = jnp.sqrt(gram_sq)
    factor = -2.0 * TOKENS * DS / (student_norm * teacher_norm[0])
    first = jnp.dot(teacher, cross.T, precision=highest, preferred_element_type=jnp.float32)
    second = jnp.dot(student, gram, precision=highest, preferred_element_type=jnp.float32)
    return factor * (first - hsic / gram_sq * second)
```

```python
import functools

import jax
import jax.numpy as jnp
from jax import lax
from jax.experimental import pallas as pl
from jax.experimental.pallas import tpu as pltpu
from jax.sharding import PartitionSpec as P

DS = 4096
TOKENS = 8192
MESH = pl.DeviceIdType.MESH
NZ = 16
TOK = 512
SC = 1024
TC = 512
CH = SC // NZ
KS = 4
KR = CH // KS
PW = 2 * CH
NP = SC // PW
OT = TOK // 8


def split(value):
    high = value.astype(jnp.bfloat16)
    return high, (value - high.astype(jnp.float32)).astype(jnp.bfloat16)


def dot3(ah, al, bh, bl, dims):
    def one(a, b):
        return lax.dot_general(a, b, (dims, ((), ())), preferred_element_type=jnp.float32)

    return one(ah, bh) + (one(ah, bl) + one(al, bh))


def kernel(
    s_ref,
    t_ref,
    tn_ref,
    out_ref,
    st_hi,
    st_lo,
    ab_hi,
    ab_lo,
    yq,
    pbuf,
    own,
    rbuf,
    full,
    opair,
    cx,
    qbuf,
    xrecv,
    stat,
    pstat,
    cstat,
    xstat,
    ystat,
    rs_send,
    rs_recv,
    ag_send,
    ag_recv,
    y_send,
    y_recv,
    p_send,
    p_recv,
    st_send,
    st_recv,
    pl_send,
    pl_recv,
    a_send,
    a_recv,
    b_send,
    b_recv,
):
    z = lax.axis_index("tok")
    y = lax.axis_index("scol")
    j = lax.axis_index("tcol")
    x = j // 2
    c = j % 2
    zdev = ({"tok": (z + 1) % NZ}, {"tok": (z + NZ - 1) % NZ})
    ydev = [{"scol": (y + d) % 4} for d in (1, 2, 3)]
    xdev = [{"tcol": ((x + d) % 4) * 2 + c} for d in (1, 2, 3)]
    sib = {"tcol": 2 * x + 1 - c}

    barrier = pltpu.get_barrier_semaphore()
    for dev in (*zdev, *ydev, *xdev, sib):
        pl.semaphore_signal(barrier, inc=1, device_id=dev, device_id_type=MESH)

    def rcopy(src, dst, ssem, rsem, dev):
        return pltpu.make_async_remote_copy(
            src_ref=src, dst_ref=dst, send_sem=ssem, recv_sem=rsem, device_id=dev, device_id_type=MESH
        )

    def rows(o, k):
        return pl.ds(pl.multiple_of(o * CH + k * KR, KR), KR)

    def rs_first(ph, d, k):
        o = (z + 8) % NZ
        return rcopy(
            own.at[ph, rows(o, k)],
            rbuf.at[ph, d, 0, pl.ds(k * KR, KR)],
            rs_send.at[ph, d, 0, k],
            rs_recv.at[ph, d, 0, k],
            zdev[d],
        )

    def rs_copy(ph, d, s, k):
        return rcopy(
            rbuf.at[ph, d, s - 2, pl.ds(k * KR, KR)],
            rbuf.at[ph, d, s - 1, pl.ds(k * KR, KR)],
            rs_send.at[ph, d, s - 1, k],
            rs_recv.at[ph, d, s - 1, k],
            zdev[d],
        )

    def rs_wait(ph, d, s, k):
        rcopy(
            rbuf.at[ph, d, s - 1, pl.ds(k * KR, KR)],
            rbuf.at[ph, d, s - 1, pl.ds(k * KR, KR)],
            rs_send.at[ph, d, s - 1, k],
            rs_recv.at[ph, d, s - 1, k],
            zdev[d],
        ).wait_recv()

    def main(d, k):
        return (k < KS // 2) if d == 0 else (k >= KS // 2)

    def rs_start(ph):
        for k in range(KS):
            rs_first(ph, 0 if k < KS // 2 else 1, k).start()

    def rs_step(ph, s):
        offs = ((z + 9 - s) % NZ, (z + s + 7) % NZ)
        for k in range(KS):
            for d in (0, 1):
                here = (ph, d, s - 2, pl.ds(k * KR, KR))
                mine = own[ph, rows(offs[d], k)]
                if main(d, k):
                    rs_wait(ph, d, s - 1, k)
                    rbuf[here] = rbuf[here] + mine
                else:

                    @pl.when(s > 2)
                    def _():
                        rs_wait(ph, d, s - 1, k)
                        rbuf[here] = rbuf[here] + mine

                    @pl.when(s == 2)
                    def _():
                        rbuf[here] = mine

                rs_copy(ph, d, s, k).start()

    def rs_final(ph):
        total = jnp.zeros((8, 128), jnp.float32)
        for k in range(KS):
            for d in (0, 1):
                rs_wait(ph, d, 8, k)
            at = pl.ds(k * KR, KR)
            value = own[ph, rows(z, k)] + (rbuf[ph, 0, 7, at] + rbuf[ph, 1, 7, at])
            full[ph, rows(z, k)] = value
            square = value * value
            for a in range(0, KR, 8):
                for b in range(0, TC, 128):
                    total = total + square[a : a + 8, b : b + 128]
        return total

    def ag_copy(ph, d, t, k):
        o = (z + NZ + 1 - t) % NZ if d == 0 else (z + t - 1) % NZ
        return rcopy(
            full.at[ph, rows(o, k)],
            full.at[ph, rows(o, k)],
            ag_send.at[ph, d, t - 1, k],
            ag_recv.at[ph, d, t - 1, k],
            zdev[d],
        )

    def ag_wait(ph, d, t, k):
        o = (z + NZ - t) % NZ if d == 0 else (z + t) % NZ
        rcopy(
            full.at[ph, rows(o, k)],
            full.at[ph, rows(o, k)],
            ag_send.at[ph, d, t - 1, k],
            ag_recv.at[ph, d, t - 1, k],
            zdev[d],
        ).wait_recv()

    def ag_start(ph):
        for k in range(KS):
            for d in (0, 1):
                ag_copy(ph, d, 1, k).start()

    def ag_arrive(ph, t):
        for k in range(KS):
            for d in (0, 1):
                last = 7 if main(d, k) else 6

                @pl.when(t <= last + 1)
                def _():
                    ag_wait(ph, d, t, k)

                @pl.when(t <= last)
                def _():
                    ag_copy(ph, d, t + 1, k).start()

    def products(ph, o1, o2):
        r1 = pl.ds(pl.multiple_of(o1 * CH, CH), CH)
        r2 = pl.ds(pl.multiple_of(o2 * CH, CH), CH)
        lh = jnp.concatenate([st_hi[r1], st_hi[r2]], axis=0)
        ll = jnp.concatenate([st_lo[r1], st_lo[r2]], axis=0)
        value = dot3(lh, ll, ab_hi[ph], ab_lo[ph], ((1,), (0,)))
        own[ph, r1] = value[:CH]
        own[ph, r2] = value[CH:]

    def products_at(ph, s):
        products(ph, (z + 9 - s) % NZ, (z + s + 7) % NZ)

    def pair_of(t):
        up = (z + t) % 2
        return ((up * (z + t - 1) + (1 - up) * (z + NZ - t)) % NZ) // 2

    def pair_product(ph, t):
        p = pair_of(t)
        wh, wl = split(full[ph, pl.ds(pl.multiple_of(p * PW, PW), PW)])
        value = dot3(ab_hi[ph], ab_lo[ph], wh, wl, ((1,), (1,)))
        return value.reshape(4, 2, OT, PW)

    def stat_copy(d, t):
        o = (z + NZ + 1 - t) % NZ if d == 0 else (z + t - 1) % NZ
        return rcopy(stat.at[o], stat.at[o], st_send.at[d, t - 1], st_recv.at[d, t - 1], zdev[d])

    def stat_wait(d, t):
        o = (z + NZ - t) % NZ if d == 0 else (z + t) % NZ
        rcopy(stat.at[o], stat.at[o], st_send.at[d, t - 1], st_recv.at[d, t - 1], zdev[d]).wait_recv()

    def plane_copy(i):
        if i == 0:
            return rcopy(pstat.at[0], cstat, pl_send.at[0], pl_recv.at[0], sib)
        if i < 4:
            return rcopy(pstat.at[1], xstat.at[i - 1], pl_send.at[i], pl_recv.at[i], xdev[i - 1])
        return rcopy(pstat.at[2], ystat.at[i - 4], pl_send.at[i], pl_recv.at[i], ydev[i - 4])

    def y_copy(d):
        return rcopy(
            s_ref.at[pl.ds(pl.multiple_of(x * 128, 128), 128), pl.ds(pl.multiple_of(c * TC, TC), TC)],
            yq.at[d - 1],
            y_send.at[d - 1],
            y_recv.at[d - 1],
            ydev[d - 1],
        )

    def p_copy(d, at):
        return rcopy(
            yq.at[d - 1],
            pbuf.at[pl.ds(pl.multiple_of(at * 128, 128), 128)],
            p_send.at[d - 1],
            p_recv.at[at],
            {"tcol": ((y + 4 - d) % 4) * 2 + c},
        )

    def forward(d):
        source = (y + 4 - d) % 4
        y_copy(d).wait_recv()

        @pl.when(source == x)
        def _():
            pbuf[pl.ds(pl.multiple_of(x * 128, 128), 128)] = yq[d - 1]

        @pl.when(source != x)
        def _():
            p_copy(d, x).start()

    def a_copy(q):
        return rcopy(opair.at[1, q - 1, :, 1 - c], cx.at[q - 1], a_send.at[q - 1], a_recv.at[q - 1], sib)

    def b_copy(q, d):
        return rcopy(
            qbuf.at[q - 1, (x + d) % 4],
            xrecv.at[d - 1, q - 1],
            b_send.at[d - 1, q - 1],
            b_recv.at[d - 1, q - 1],
            xdev[d - 1],
        )

    def stage_b(q):
        a_copy(q).wait_recv()
        qbuf[q - 1] = opair[1, q - 1, :, c] + cx[q - 1]
        for d in (1, 3, 2):
            b_copy(q, d).start()

    def stage_f(q):
        for d in (1, 2, 3):
            b_copy(q, d).wait_recv()
        value = (qbuf[q - 1, x] + xrecv[0, q - 1]) + (xrecv[1, q - 1] + xrecv[2, q - 1])
        p = pair_of(q)
        out_ref[:, pl.ds(pl.multiple_of(p * PW, PW), PW)] = value

    th, tl = split(t_ref[...])
    ab_hi[0] = th
    ab_lo[0] = tl
    for a in range(0, SC, 256):
        sh, sl = split(s_ref[:, a : a + 256].T)
        st_hi[a : a + 256] = sh
        st_lo[a : a + 256] = sl
    pl.semaphore_wait(barrier, 9)
    for d in (1, 3, 2):
        y_copy(d).start()

    products(0, (z + 8) % NZ, z)
    rs_start(0)

    @pl.loop(2, 9)
    def _(s):
        products_at(0, s)
        rs_step(0, s)

        @pl.when(s == 5)
        def _():
            forward(1)
            forward(3)

        @pl.when(s == 7)
        def _():
            forward(2)

    @pl.when(x == y)
    def _():
        pbuf[...] = s_ref[:, pl.ds(pl.multiple_of(c * TC, TC), TC)]

    @pl.when(x != y)
    def _():
        for e in (1, 2, 3):
            p_copy(1, (x + e) % 4).wait_recv()

    ph_, pl_ = split(pbuf[...])
    ab_hi[1] = ph_
    ab_lo[1] = pl_
    products(1, (z + 8) % NZ, z)
    rs_start(1)
    stat[z, :8] = rs_final(0)

    @pl.loop(2, 9)
    def _(s):
        products_at(1, s)
        rs_step(1, s)

    ag_start(0)
    stat[z, 8:] = rs_final(1)
    for d in (0, 1):
        stat_copy(d, 1).start()

    @pl.loop(1, 9)
    def _(t):
        @pl.when(t == 8)
        def _():
            ag_start(1)

        ag_arrive(0, t)
        for d in (0, 1):
            last = 8 if d == 0 else 7

            @pl.when(t <= last)
            def _():
                stat_wait(d, t)

            @pl.when(t < last)
            def _():
                stat_copy(d, t + 1).start()

        opair[0, t - 1] = pair_product(0, t)

    total = stat[0]
    for o in range(1, NZ):
        total = total + stat[o]
    pstat[0] = total
    plane_copy(0).start()

    @pl.loop(1, 9)
    def _(t):
        ag_arrive(1, t)
        opair[1, t - 1] = pair_product(1, t)

        @pl.when(t == 1)
        def _():
            plane_copy(0).wait_recv()
            pstat[1] = pstat[0] + cstat[...]
            for i in (1, 2, 3):
                plane_copy(i).start()

        @pl.when(t == 2)
        def _():
            for i in (1, 2, 3):
                plane_copy(i).wait_recv()
            pstat[2] = (pstat[1] + xstat[0]) + (xstat[1] + xstat[2])
            for i in (4, 5, 6):
                plane_copy(i).start()

        @pl.when(t == 3)
        def _():
            for i in (4, 5, 6):
                plane_copy(i).wait_recv()
            value = (pstat[2] + ystat[0]) + (ystat[1] + ystat[2])
            hsic = jnp.sum(value[:8], keepdims=True)
            gram_sq = jnp.sum(value[8:], keepdims=True)
            factor = -2.0 * TOKENS * DS / (jnp.sqrt(gram_sq) * tn_ref[0])
            ratio = hsic / gram_sq
            pstat[3, :8] = jnp.broadcast_to(factor, (8, 128))
            pstat[3, 8:] = jnp.broadcast_to(ratio, (8, 128))

        def finish(q):
            factor = pstat[3, 0:1]
            ratio = pstat[3, 8:9]
            opair[1, q - 1] = factor * (opair[0, q - 1] - ratio * opair[1, q - 1])
            a_copy(q).start()

        @pl.when(t == 4)
        def _():
            pl.loop(1, 4)(finish)

        @pl.when(t >= 4)
        def _():
            finish(t)

        @pl.when(t == 5)
        def _():
            pl.loop(1, 4)(stage_b)

        @pl.when(t >= 5)
        def _():
            stage_b(t - 1)

        @pl.when(t == 6)
        def _():
            pl.loop(1, 4)(stage_f)

        @pl.when(t >= 6)
        def _():
            stage_f(t - 2)

    stage_b(8)
    stage_f(7)
    stage_f(8)

    for d in (1, 2, 3):
        y_copy(d).wait_send()

        @pl.when((y + 4 - d) % 4 != x)
        def _():
            p_copy(d, x).wait_send()

    for ph in (0, 1):
        for k in range(KS):
            rs_first(ph, 0 if k < KS // 2 else 1, k).wait_send()

        @pl.loop(2, 9)
        def _(s):
            for k in range(KS):
                for d in (0, 1):
                    rs_copy(ph, d, s, k).wait_send()

        @pl.loop(1, 9)
        def _(t):
            for k in range(KS):
                for d in (0, 1):
                    last = 8 if main(d, k) else 7

                    @pl.when(t <= last)
                    def _():
                        ag_copy(ph, d, t, k).wait_send()

    @pl.loop(1, 9)
    def _(t):
        stat_copy(0, t).wait_send()

        @pl.when(t < 8)
        def _():
            stat_copy(1, t).wait_send()

        a_copy(t).wait_send()
        for d in (1, 2, 3):
            b_copy(t, d).wait_send()

    for i in range(7):
        plane_copy(i).wait_send()


def body(student, teacher, teacher_norm):
    f32, bf16 = jnp.float32, jnp.bfloat16
    dma = pltpu.SemaphoreType.DMA
    return pl.pallas_call(
        kernel,
        out_shape=jax.ShapeDtypeStruct((OT, SC), f32),
        in_specs=[
            pl.BlockSpec(memory_space=pltpu.VMEM),
            pl.BlockSpec(memory_space=pltpu.VMEM),
            pl.BlockSpec(memory_space=pltpu.SMEM),
        ],
        out_specs=pl.BlockSpec(memory_space=pltpu.VMEM),
        scratch_shapes=[
            pltpu.VMEM((SC, TOK), bf16),
            pltpu.VMEM((SC, TOK), bf16),
            pltpu.VMEM((2, TOK, TC), bf16),
            pltpu.VMEM((2, TOK, TC), bf16),
            pltpu.VMEM((3, 128, TC), f32),
            pltpu.VMEM((TOK, TC), f32),
            pltpu.VMEM((2, SC, TC), f32),
            pltpu.VMEM((2, 2, 8, CH, TC), f32),
            pltpu.VMEM((2, SC, TC), f32),
            pltpu.VMEM((2, NP, 4, 2, OT, PW), f32),
            pltpu.VMEM((NP, 4, OT, PW), f32),
            pltpu.VMEM((NP, 4, OT, PW), f32),
            pltpu.VMEM((3, NP, OT, PW), f32),
            pltpu.VMEM((NZ, 16, 128), f32),
            pltpu.VMEM((4, 16, 128), f32),
            pltpu.VMEM((16, 128), f32),
            pltpu.VMEM((3, 16, 128), f32),
            pltpu.VMEM((3, 16, 128), f32),
            dma((2, 2, 8, KS)),
            dma((2, 2, 8, KS)),
            dma((2, 2, 8, KS)),
            dma((2, 2, 8, KS)),
            dma((3,)),
            dma((3,)),
            dma((3,)),
            dma((4,)),
            dma((2, 8)),
            dma((2, 8)),
            dma((7,)),
            dma((7,)),
            dma((8,)),
            dma((8,)),
            dma((3, 8)),
            dma((3, 8)),
        ],
        compiler_params=pltpu.CompilerParams(
            collective_id=0, has_side_effects=True, vmem_limit_bytes=48 * 1024 * 1024
        ),
    )(student, teacher, teacher_norm)


def solution(mesh):
    return jax.shard_map(
        body,
        mesh=mesh,
        in_specs=(P("tok", "scol"), P("tok", "tcol"), P()),
        out_specs=P(("tok", "tcol"), "scol"),
        check_vma=False,
    )
```

```python
import functools

import jax
import jax.numpy as jnp
from jax import lax
from jax.experimental import pallas as pl
from jax.experimental.pallas import tpu as pltpu
from jax.sharding import PartitionSpec as P

DS = 4096
TOKENS = 8192
MESH = pl.DeviceIdType.MESH
NZ = 16
TOK = 512
SC = 1024
TC = 512
CH = SC // NZ
KS = 4
KR = CH // KS
PW = 2 * CH
NP = SC // PW
OT = TOK // 8


def split(value):
    high = value.astype(jnp.bfloat16)
    return high, (value - high.astype(jnp.float32)).astype(jnp.bfloat16)


def dot3(ah, al, bh, bl, dims):
    def one(a, b):
        return lax.dot_general(a, b, (dims, ((), ())), preferred_element_type=jnp.float32)

    return one(ah, bh) + (one(ah, bl) + one(al, bh))


def kernel(
    s_ref,
    t_ref,
    tn_ref,
    out_ref,
    st_hi,
    st_lo,
    ab_hi,
    ab_lo,
    yq,
    pbuf,
    own,
    rbuf,
    full,
    opair,
    cx,
    qbuf,
    xrecv,
    zstat,
    tstat,
    ystat,
    scale,
    rs_send,
    rs_recv,
    ag_send,
    ag_recv,
    y_send,
    y_recv,
    p_send,
    p_recv,
    st_send,
    st_recv,
    ts_send,
    ts_recv,
    ys_send,
    ys_recv,
    a_send,
    a_recv,
    b_send,
    b_recv,
):
    z = lax.axis_index("tok")
    y = lax.axis_index("scol")
    j = lax.axis_index("tcol")
    x = j // 2
    c = j % 2
    zdev = ({"tok": (z + 1) % NZ}, {"tok": (z + NZ - 1) % NZ})
    ydev = [{"scol": (y + d) % 4} for d in (1, 2, 3)]
    xdev = [{"tcol": ((x + d) % 4) * 2 + c} for d in (1, 2, 3)]
    sib = {"tcol": 2 * x + 1 - c}
    tdev = [{"tcol": (j + e) % 8} for e in range(1, 8)]

    barrier = pltpu.get_barrier_semaphore()
    for dev in (*zdev, *ydev, *tdev):
        pl.semaphore_signal(barrier, inc=1, device_id=dev, device_id_type=MESH)

    def rcopy(src, dst, ssem, rsem, dev):
        return pltpu.make_async_remote_copy(
            src_ref=src, dst_ref=dst, send_sem=ssem, recv_sem=rsem, device_id=dev, device_id_type=MESH
        )

    def rows(o, k):
        return pl.ds(pl.multiple_of(o * CH + k * KR, KR), KR)

    def rs_first(ph, d, k):
        o = (z + 8) % NZ
        return rcopy(
            own.at[ph, rows(o, k)],
            rbuf.at[ph, d, 0, pl.ds(k * KR, KR)],
            rs_send.at[ph, d, k],
            rs_recv.at[ph, d, 0, k],
            zdev[d],
        )

    def rs_copy(ph, d, s, k):
        return rcopy(
            rbuf.at[ph, d, s - 2, pl.ds(k * KR, KR)],
            rbuf.at[ph, d, s - 1, pl.ds(k * KR, KR)],
            rs_send.at[ph, d, k],
            rs_recv.at[ph, d, s - 1, k],
            zdev[d],
        )

    def rs_wait(ph, d, s, k):
        rcopy(
            rbuf.at[ph, d, s - 1, pl.ds(k * KR, KR)],
            rbuf.at[ph, d, s - 1, pl.ds(k * KR, KR)],
            rs_send.at[ph, d, k],
            rs_recv.at[ph, d, s - 1, k],
            zdev[d],
        ).wait_recv()

    def main(d, k):
        return (k < KS // 2) if d == 0 else (k >= KS // 2)

    def rs_second(ph, d, k):
        o = (z + 7) % NZ if d == 0 else (z + 9) % NZ
        return rcopy(
            own.at[ph, rows(o, k)],
            rbuf.at[ph, d, 1, pl.ds(k * KR, KR)],
            rs_send.at[ph, d, k],
            rs_recv.at[ph, d, 1, k],
            zdev[d],
        )

    def rs_start(ph):
        products(ph, (z + 8) % NZ, z)
        for k in range(KS):
            rs_first(ph, 0 if k < KS // 2 else 1, k).start()
        products_at(ph, 2)
        for k in range(KS):
            rs_second(ph, 1 if k < KS // 2 else 0, k).start()

    def rs_step(ph, s, only_main=False):
        offs = ((z + 9 - s) % NZ, (z + s + 7) % NZ)
        for k in range(KS):
            for d in (0, 1):
                if only_main and not main(d, k):
                    continue
                here = (ph, d, s - 2, pl.ds(k * KR, KR))
                mine = own[ph, rows(offs[d], k)]
                rs_wait(ph, d, s - 1, k)
                rbuf[here] = rbuf[here] + mine
                rs_copy(ph, d, s, k).start()

    def rs_final(ph):
        total = jnp.zeros((8, 128), jnp.float32)
        for k in range(KS):
            for d in (0, 1):
                rs_wait(ph, d, 8, k)
            at = pl.ds(k * KR, KR)
            value = own[ph, rows(z, k)] + (rbuf[ph, 0, 7, at] + rbuf[ph, 1, 7, at])
            full[ph, rows(z, k)] = value
            square = value * value
            for a in range(0, KR, 8):
                for b in range(0, TC, 128):
                    total = total + square[a : a + 8, b : b + 128]
        zstat[z, :, ph * 128 : ph * 128 + 128] = jnp.sum(total, axis=0, keepdims=True)

    def ag_copy(ph, d, t, k):
        o = (z + NZ + 1 - t) % NZ if d == 0 else (z + t - 1) % NZ
        return rcopy(
            full.at[ph, rows(o, k)],
            full.at[ph, rows(o, k)],
            ag_send.at[ph, d, k],
            ag_recv.at[ph, d, t - 1, k],
            zdev[d],
        )

    def ag_wait(ph, d, t, k):
        o = (z + NZ - t) % NZ if d == 0 else (z + t) % NZ
        rcopy(
            full.at[ph, rows(o, k)],
            full.at[ph, rows(o, k)],
            ag_send.at[ph, d, k],
            ag_recv.at[ph, d, t - 1, k],
            zdev[d],
        ).wait_recv()

    def ag_start(ph):
        for k in range(KS):
            for d in (0, 1):
                ag_copy(ph, d, 1, k).start()

    def ag_arrive(ph, t, last=6):
        for k in range(KS):
            for d in (0, 1):
                if last < 8 or main(d, k):
                    ag_wait(ph, d, t, k)
                if last < 7 or (last == 7 and main(d, k)):
                    ag_copy(ph, d, t + 1, k).start()

    def products(ph, o1, o2):
        r1 = pl.ds(pl.multiple_of(o1 * CH, CH), CH)
        r2 = pl.ds(pl.multiple_of(o2 * CH, CH), CH)
        lh = jnp.concatenate([st_hi[r1], st_hi[r2]], axis=0)
        ll = jnp.concatenate([st_lo[r1], st_lo[r2]], axis=0)
        value = dot3(lh, ll, ab_hi[ph], ab_lo[ph], ((1,), (0,)))
        own[ph, r1] = value[:CH]
        own[ph, r2] = value[CH:]

    def products_at(ph, s):
        products(ph, (z + 9 - s) % NZ, (z + s + 7) % NZ)

    def pair_of(t):
        up = (z + t) % 2
        return ((up * (z + t - 1) + (1 - up) * (z + NZ - t)) % NZ) // 2

    def pair_product(ph, t):
        p = pair_of(t)
        wh, wl = split(full[ph, pl.ds(pl.multiple_of(p * PW, PW), PW)])
        value = dot3(ab_hi[ph], ab_lo[ph], wh, wl, ((1,), (1,)))
        return value.reshape(4, 2, OT, PW)

    def zs_copy(e):
        return rcopy(zstat.at[z], zstat.at[z], st_send, st_recv, {"tok": (z + e) % NZ})

    def zs_all():
        part = zstat.at[pl.ds(0, NZ - 1)]
        return rcopy(part, part, st_send, st_recv, zdev[0])

    def ts_copy(e):
        return rcopy(tstat.at[j], tstat.at[j], ts_send, ts_recv, tdev[e - 1])

    def ts_all():
        part = tstat.at[pl.ds(0, 7)]
        return rcopy(part, part, ts_send, ts_recv, tdev[0])

    def ys_copy(e):
        return rcopy(ystat.at[y], ystat.at[y], ys_send, ys_recv, ydev[e - 1])

    def ys_all():
        part = ystat.at[pl.ds(0, 3)]
        return rcopy(part, part, ys_send, ys_recv, ydev[0])

    def y_copy(d):
        return rcopy(
            s_ref.at[pl.ds(pl.multiple_of(x * 128, 128), 128), pl.ds(pl.multiple_of(c * TC, TC), TC)],
            yq.at[d - 1],
            y_send.at[d - 1],
            y_recv.at[d - 1],
            ydev[d - 1],
        )

    def p_copy(d, at):
        return rcopy(
            yq.at[d - 1],
            pbuf.at[pl.ds(pl.multiple_of(at * 128, 128), 128)],
            p_send.at[d - 1],
            p_recv.at[at],
            {"tcol": ((y + 4 - d) % 4) * 2 + c},
        )

    def forward(d):
        source = (y + 4 - d) % 4
        y_copy(d).wait_recv()

        @pl.when(source == x)
        def _():
            pbuf[pl.ds(pl.multiple_of(x * 128, 128), 128)] = yq[d - 1]

        @pl.when(source != x)
        def _():
            p_copy(d, x).start()

    def a_copy(q):
        return rcopy(opair.at[1, q - 1, :, 1 - c], cx.at[q - 1], a_send, a_recv.at[q - 1], sib)

    def b_copy(q, d):
        return rcopy(
            qbuf.at[q - 1, (x + d) % 4],
            xrecv.at[d - 1, q - 1],
            b_send.at[d - 1],
            b_recv.at[d - 1, q - 1],
            xdev[d - 1],
        )

    def stage_b(q):
        a_copy(q).wait_recv()
        qbuf[q - 1] = opair[1, q - 1, :, c] + cx[q - 1]
        for d in (1, 3, 2):
            b_copy(q, d).start()

    def stage_f(q):
        for d in (1, 2, 3):
            b_copy(q, d).wait_recv()
        value = (qbuf[q - 1, x] + xrecv[0, q - 1]) + (xrecv[1, q - 1] + xrecv[2, q - 1])
        p = pair_of(q)
        out_ref[:, pl.ds(pl.multiple_of(p * PW, PW), PW)] = value

    th, tl = split(t_ref[...])
    ab_hi[0] = th
    ab_lo[0] = tl
    for a in range(0, SC, 256):
        sh, sl = split(s_ref[:, a : a + 256].T)
        st_hi[a : a + 256] = sh
        st_lo[a : a + 256] = sl
    pl.semaphore_wait(barrier, 12)
    for d in (1, 3, 2):
        y_copy(d).start()

    rs_start(0)
    products_at(0, 3)
    rs_step(0, 2, True)

    @pl.loop(3, 9)
    def _(s):
        @pl.when(s < 8)
        def _():
            products_at(0, s + 1)

        rs_step(0, s)

        @pl.when(s == 3)
        def _():
            forward(1)
            forward(3)

        @pl.when(s == 5)
        def _():
            forward(2)

    rs_final(0)
    ag_start(0)

    @pl.when(x == y)
    def _():
        pbuf[...] = s_ref[:, pl.ds(pl.multiple_of(c * TC, TC), TC)]

    @pl.when(x != y)
    def _():
        for e in (1, 2, 3):
            p_copy(1, (x + e) % 4).wait_recv()

    gh, gl = split(pbuf[...])
    ab_hi[1] = gh
    ab_lo[1] = gl
    rs_start(1)

    def both(s, t_last=6, only_main=False):
        ag_arrive(0, s - 1, t_last)
        rs_step(1, s, only_main)
        opair[0, s - 2] = pair_product(0, s - 1)

    products_at(1, 3)
    both(2, 6, True)

    @pl.loop(3, 8)
    def _(s):
        products_at(1, s + 1)
        both(s)

    both(8, 7)
    rs_final(1)

    @pl.loop(1, NZ)
    def _(e):
        zs_copy(e).start()

    ag_start(1)
    ag_arrive(0, 8, 8)
    opair[0, 7] = pair_product(0, 8)

    def finish(q):
        opair[1, q - 1] = scale[0:1] * (opair[0, q - 1] - scale[1:2] * opair[1, q - 1])
        a_copy(q).start()

    @pl.loop(1, 7)
    def _(t):
        ag_arrive(1, t)
        opair[1, t - 1] = pair_product(1, t)

        @pl.when(t == 2)
        def _():
            zs_all().wait_recv()
            total = zstat[0]
            for o in range(1, NZ):
                total = total + zstat[o]
            tstat[j] = total
            for e in range(1, 8):
                ts_copy(e).start()

        @pl.when(t == 3)
        def _():
            ts_all().wait_recv()
            total = tstat[0]
            for o in range(1, 8):
                total = total + tstat[o]
            ystat[y] = total
            for e in (1, 2, 3):
                ys_copy(e).start()

        @pl.when(t == 4)
        def _():
            ys_all().wait_recv()
            total = (ystat[0] + ystat[1]) + (ystat[2] + ystat[3])
            hsic = jnp.sum(total[:, :128], keepdims=True)
            gram_sq = jnp.sum(total[:, 128:], keepdims=True)
            factor = -2.0 * TOKENS * DS / (jnp.sqrt(gram_sq) * tn_ref[0])
            scale[0:1] = jnp.broadcast_to(factor, (1, 128))
            scale[1:2] = jnp.broadcast_to(hsic / gram_sq, (1, 128))
            pl.loop(1, 5)(finish)

        @pl.when(t == 5)
        def _():
            pl.loop(1, 5)(stage_b)
            finish(5)

        @pl.when(t == 6)
        def _():
            finish(6)
            stage_b(5)

    ag_arrive(1, 7, 7)
    opair[1, 6] = pair_product(1, 7)
    finish(7)
    stage_b(6)
    ag_arrive(1, 8, 8)
    opair[1, 7] = pair_product(1, 8)
    finish(8)
    stage_b(7)
    pl.loop(1, 6)(stage_f)
    stage_b(8)
    pl.loop(6, 9)(stage_f)

    for d in (1, 2, 3):
        y_copy(d).wait_send()

        @pl.when((y + 4 - d) % 4 != x)
        def _():
            p_copy(d, x).wait_send()

    for ph in (0, 1):
        for k in range(KS):
            for d in (0, 1):
                sent = rbuf.at[ph, d, pl.ds(0, 8 if main(d, k) else 7), pl.ds(k * KR, KR)]
                rcopy(sent, sent, rs_send.at[ph, d, k], rs_recv.at[ph, d, 0, k], zdev[d]).wait_send()
                rcopy(sent, sent, ag_send.at[ph, d, k], ag_recv.at[ph, d, 0, k], zdev[d]).wait_send()

    zs_all().wait_send()
    ts_all().wait_send()
    ys_all().wait_send()
    rcopy(cx, cx, a_send, a_recv.at[0], sib).wait_send()
    for d in (1, 2, 3):
        rcopy(xrecv.at[d - 1], xrecv.at[d - 1], b_send.at[d - 1], b_recv.at[d - 1, 0], xdev[d - 1]).wait_send()


def body(student, teacher, teacher_norm):
    f32, bf16 = jnp.float32, jnp.bfloat16
    dma = pltpu.SemaphoreType.DMA
    return pl.pallas_call(
        kernel,
        out_shape=jax.ShapeDtypeStruct((OT, SC), f32),
        in_specs=[
            pl.BlockSpec(memory_space=pltpu.VMEM),
            pl.BlockSpec(memory_space=pltpu.VMEM),
            pl.BlockSpec(memory_space=pltpu.SMEM),
        ],
        out_specs=pl.BlockSpec(memory_space=pltpu.VMEM),
        scratch_shapes=[
            pltpu.VMEM((SC, TOK), bf16),
            pltpu.VMEM((SC, TOK), bf16),
            pltpu.VMEM((2, TOK, TC), bf16),
            pltpu.VMEM((2, TOK, TC), bf16),
            pltpu.VMEM((3, 128, TC), f32),
            pltpu.VMEM((TOK, TC), f32),
            pltpu.VMEM((2, SC, TC), f32),
            pltpu.VMEM((2, 2, 8, CH, TC), f32),
            pltpu.VMEM((2, SC, TC), f32),
            pltpu.VMEM((2, NP, 4, 2, OT, PW), f32),
            pltpu.VMEM((NP, 4, OT, PW), f32),
            pltpu.VMEM((NP, 4, OT, PW), f32),
            pltpu.VMEM((3, NP, OT, PW), f32),
            pltpu.VMEM((NZ, 1, 256), f32),
            pltpu.VMEM((8, 1, 256), f32),
            pltpu.VMEM((4, 1, 256), f32),
            pltpu.VMEM((8, 128), f32),
            dma((2, 2, KS)),
            dma((2, 2, 8, KS)),
            dma((2, 2, KS)),
            dma((2, 2, 8, KS)),
            dma((3,)),
            dma((3,)),
            dma((3,)),
            dma((4,)),
            dma,
            dma,
            dma,
            dma,
            dma,
            dma,
            dma,
            dma((8,)),
            dma((3,)),
            dma((3, 8)),
        ],
        compiler_params=pltpu.CompilerParams(
            collective_id=0, has_side_effects=True, vmem_limit_bytes=48 * 1024 * 1024
        ),
    )(student, teacher, teacher_norm)


def solution(mesh):
    return jax.shard_map(
        body,
        mesh=mesh,
        in_specs=(P("tok", "scol"), P("tok", "tcol"), P()),
        out_specs=P(("tok", "tcol"), "scol"),
        check_vma=False,
    )
```

```python
import functools

import jax
import jax.numpy as jnp
from jax import lax
from jax.experimental import pallas as pl
from jax.experimental.pallas import tpu as pltpu
from jax.sharding import PartitionSpec as P

DS = 4096
TOKENS = 8192
MESH = pl.DeviceIdType.MESH
NZ = 16
TOK = 512
SC = 1024
TC = 512
CH = SC // NZ
KS = 4
KR = CH // KS
PW = 2 * CH
NP = SC // PW
OT = TOK // 8


def split(value):
    high = value.astype(jnp.bfloat16)
    return high, (value - high.astype(jnp.float32)).astype(jnp.bfloat16)


def dot3(ah, al, bh, bl, dims):
    def one(a, b):
        return lax.dot_general(a, b, (dims, ((), ())), preferred_element_type=jnp.float32)

    return one(ah, bh) + (one(ah, bl) + one(al, bh))


def kernel(
    s_ref,
    t_ref,
    tn_ref,
    out_ref,
    sbuf,
    tbuf,
    load_sem,
    st_hi,
    st_lo,
    ab_hi,
    ab_lo,
    yq,
    pbuf,
    own,
    rbuf,
    full,
    opair,
    cx,
    qbuf,
    xrecv,
    zstat,
    tstat,
    ystat,
    scale,
    rs_send,
    rs_recv,
    ag_send,
    ag_recv,
    y_send,
    y_recv,
    p_send,
    p_recv,
    st_send,
    st_recv,
    ts_send,
    ts_recv,
    ys_send,
    ys_recv,
    a_send,
    a_recv,
    b_send,
    b_recv,
):
    z = lax.axis_index("tok")
    y = lax.axis_index("scol")
    j = lax.axis_index("tcol")
    x = j // 2
    c = j % 2
    zdev = ({"tok": (z + 1) % NZ}, {"tok": (z + NZ - 1) % NZ})
    ydev = [{"scol": (y + d) % 4} for d in (1, 2, 3)]
    xdev = [{"tcol": ((x + d) % 4) * 2 + c} for d in (1, 2, 3)]
    sib = {"tcol": 2 * x + 1 - c}
    tdev = [{"tcol": (j + e) % 8} for e in range(1, 8)]

    barrier = pltpu.get_barrier_semaphore()
    for dev in (*zdev, *ydev, *tdev):
        pl.semaphore_signal(barrier, inc=1, device_id=dev, device_id_type=MESH)

    def rcopy(src, dst, ssem, rsem, dev):
        return pltpu.make_async_remote_copy(
            src_ref=src, dst_ref=dst, send_sem=ssem, recv_sem=rsem, device_id=dev, device_id_type=MESH
        )

    def rows(o, k):
        return pl.ds(pl.multiple_of(o * CH + k * KR, KR), KR)

    def rs_first(ph, d, k):
        o = (z + 8) % NZ
        return rcopy(
            own.at[ph, rows(o, k)],
            rbuf.at[ph, d, 0, pl.ds(k * KR, KR)],
            rs_send.at[ph, d, k],
            rs_recv.at[ph, d, 0, k],
            zdev[d],
        )

    def rs_copy(ph, d, s, k):
        return rcopy(
            rbuf.at[ph, d, s - 2, pl.ds(k * KR, KR)],
            rbuf.at[ph, d, s - 1, pl.ds(k * KR, KR)],
            rs_send.at[ph, d, k],
            rs_recv.at[ph, d, s - 1, k],
            zdev[d],
        )

    def rs_wait(ph, d, s, k):
        rcopy(
            rbuf.at[ph, d, s - 1, pl.ds(k * KR, KR)],
            rbuf.at[ph, d, s - 1, pl.ds(k * KR, KR)],
            rs_send.at[ph, d, k],
            rs_recv.at[ph, d, s - 1, k],
            zdev[d],
        ).wait_recv()

    def main(d, k):
        return (k < KS // 2) if d == 0 else (k >= KS // 2)

    def rs_second(ph, d, k):
        o = (z + 7) % NZ if d == 0 else (z + 9) % NZ
        return rcopy(
            own.at[ph, rows(o, k)],
            rbuf.at[ph, d, 1, pl.ds(k * KR, KR)],
            rs_send.at[ph, d, k],
            rs_recv.at[ph, d, 1, k],
            zdev[d],
        )

    def rs_start(ph):
        for k in range(KS):
            rs_first(ph, 0 if k < KS // 2 else 1, k).start()
        if ph == 0:
            prepare(2)
        products(ph, 2)
        for k in range(KS):
            rs_second(ph, 1 if k < KS // 2 else 0, k).start()

    def rs_step(ph, s, only_main=False):
        offs = ((z + 9 - s) % NZ, (z + s + 7) % NZ)
        for k in range(KS):
            for d in (0, 1):
                if only_main and not main(d, k):
                    continue
                here = (ph, d, s - 2, pl.ds(k * KR, KR))
                mine = own[ph, rows(offs[d], k)]
                rs_wait(ph, d, s - 1, k)
                rbuf[here] = rbuf[here] + mine
                rs_copy(ph, d, s, k).start()

    def rs_final(ph):
        total = jnp.zeros((8, 128), jnp.float32)
        for k in range(KS):
            for d in (0, 1):
                rs_wait(ph, d, 8, k)
            at = pl.ds(k * KR, KR)
            value = own[ph, rows(z, k)] + (rbuf[ph, 0, 7, at] + rbuf[ph, 1, 7, at])
            full[ph, rows(z, k)] = value
            square = value * value
            for a in range(0, KR, 8):
                for b in range(0, TC, 128):
                    total = total + square[a : a + 8, b : b + 128]
            if k < KS - 1:
                for d in (0, 1):
                    ag_copy(ph, d, 1, k).start()
        zstat[z, :, ph * 128 : ph * 128 + 128] = jnp.sum(total, axis=0, keepdims=True)
        if ph == 1:
            for e in range(1, NZ):
                zs_copy(e).start()
        for d in (0, 1):
            ag_copy(ph, d, 1, KS - 1).start()

    def ag_copy(ph, d, t, k):
        o = (z + NZ + 1 - t) % NZ if d == 0 else (z + t - 1) % NZ
        return rcopy(
            full.at[ph, rows(o, k)],
            full.at[ph, rows(o, k)],
            ag_send.at[ph, d, k],
            ag_recv.at[ph, d, t - 1, k],
            zdev[d],
        )

    def ag_wait(ph, d, t, k):
        o = (z + NZ - t) % NZ if d == 0 else (z + t) % NZ
        rcopy(
            full.at[ph, rows(o, k)],
            full.at[ph, rows(o, k)],
            ag_send.at[ph, d, k],
            ag_recv.at[ph, d, t - 1, k],
            zdev[d],
        ).wait_recv()

    def ag_arrive(ph, t, last=6):
        for k in range(KS):
            for d in (0, 1):
                if last < 8 or main(d, k):
                    ag_wait(ph, d, t, k)
                if last < 7 or (last == 7 and main(d, k)):
                    ag_copy(ph, d, t + 1, k).start()

    def block_of(s):
        up = (z + s) % 2
        p = ((up * (z + 7 + s) + (1 - up) * (z + 9 - s)) % NZ) // 2
        return pl.ds(pl.multiple_of(p * PW, PW), PW)

    def prepare(s):
        at = block_of(s)
        sh, sl = split(sbuf[:, at].T)
        st_hi[at] = sh
        st_lo[at] = sl

    def products(ph, s):
        at = block_of(s)
        own[ph, at] = dot3(st_hi[at], st_lo[at], ab_hi[ph], ab_lo[ph], ((1,), (0,)))

    def pair_of(t):
        up = (z + t) % 2
        return ((up * (z + t - 1) + (1 - up) * (z + NZ - t)) % NZ) // 2

    def pair_product(ph, t):
        p = pair_of(t)
        wh, wl = split(full[ph, pl.ds(pl.multiple_of(p * PW, PW), PW)])

        def one(a, b):
            return lax.dot_general(a, b, (((1,), (1,)), ((), ())), preferred_element_type=jnp.float32)

        wide = one(ab_hi[ph], jnp.concatenate([wh, wl], axis=0))
        value = wide[:, :PW] + (wide[:, PW:] + one(ab_lo[ph], wh))
        return value.reshape(4, 2, OT, PW)

    def zs_copy(e):
        return rcopy(zstat.at[z], zstat.at[z], st_send, st_recv, {"tok": (z + e) % NZ})

    def zs_all():
        part = zstat.at[pl.ds(0, NZ - 1)]
        return rcopy(part, part, st_send, st_recv, zdev[0])

    def ts_copy(e):
        return rcopy(tstat.at[j], tstat.at[j], ts_send, ts_recv, tdev[e - 1])

    def ts_all():
        part = tstat.at[pl.ds(0, 7)]
        return rcopy(part, part, ts_send, ts_recv, tdev[0])

    def ys_copy(e):
        return rcopy(ystat.at[y], ystat.at[y], ys_send, ys_recv, ydev[e - 1])

    def ys_all():
        part = ystat.at[pl.ds(0, 3)]
        return rcopy(part, part, ys_send, ys_recv, ydev[0])

    def y_copy(d):
        return rcopy(
            sbuf.at[pl.ds(pl.multiple_of(x * 128, 128), 128), pl.ds(pl.multiple_of(c * TC, TC), TC)],
            yq.at[d - 1],
            y_send.at[d - 1],
            y_recv.at[d - 1],
            ydev[d - 1],
        )

    def p_copy(d, at):
        return rcopy(
            yq.at[d - 1],
            pbuf.at[pl.ds(pl.multiple_of(at * 128, 128), 128)],
            p_send.at[d - 1],
            p_recv.at[at],
            {"tcol": ((y + 4 - d) % 4) * 2 + c},
        )

    def forward(d):
        source = (y + 4 - d) % 4
        y_copy(d).wait_recv()

        @pl.when(source == x)
        def _():
            pbuf[pl.ds(pl.multiple_of(x * 128, 128), 128)] = yq[d - 1]

        @pl.when(source != x)
        def _():
            p_copy(d, x).start()

    def a_copy(q):
        return rcopy(opair.at[1, q - 1, :, 1 - c], cx.at[q - 1], a_send, a_recv.at[q - 1], sib)

    def b_copy(q, d):
        return rcopy(
            qbuf.at[q - 1, (x + d) % 4],
            xrecv.at[d - 1, q - 1],
            b_send.at[d - 1],
            b_recv.at[d - 1, q - 1],
            xdev[d - 1],
        )

    def stage_b(q):
        a_copy(q).wait_recv()
        qbuf[q - 1] = opair[1, q - 1, :, c] + cx[q - 1]
        for d in (1, 3, 2):
            b_copy(q, d).start()

    def stage_f(q):
        for d in (1, 2, 3):
            b_copy(q, d).wait_recv()
        value = (qbuf[q - 1, x] + xrecv[0, q - 1]) + (xrecv[1, q - 1] + xrecv[2, q - 1])
        p = pair_of(q)
        out_ref[:, pl.ds(pl.multiple_of(p * PW, PW), PW)] = value

    loads = [pltpu.make_async_copy(t_ref, tbuf, load_sem.at[0]), pltpu.make_async_copy(s_ref, sbuf, load_sem.at[1])]
    for load in loads:
        load.start()
    loads[0].wait()
    th, tl = split(tbuf[...])
    ab_hi[0] = th
    ab_lo[0] = tl
    loads[1].wait()
    prepare(1)
    products(0, 1)
    pl.semaphore_wait(barrier, 12)
    for d in (1, 3, 2):
        y_copy(d).start()

    rs_start(0)
    prepare(3)
    products(0, 3)
    rs_step(0, 2, True)

    @pl.loop(3, 9)
    def _(s):
        @pl.when(s < 8)
        def _():
            prepare(s + 1)
            products(0, s + 1)

        rs_step(0, s)

        @pl.when(s == 3)
        def _():
            forward(1)
            forward(3)

        @pl.when(s == 5)
        def _():
            forward(2)

    rs_final(0)

    @pl.when(x == y)
    def _():
        pbuf[...] = sbuf[:, pl.ds(pl.multiple_of(c * TC, TC), TC)]

    @pl.when(x != y)
    def _():
        for e in (1, 2, 3):
            p_copy(1, (x + e) % 4).wait_recv()

    gh, gl = split(pbuf[...])
    ab_hi[1] = gh
    ab_lo[1] = gl
    products(1, 1)
    rs_start(1)

    def both(s, t_last=6, only_main=False):
        ag_arrive(0, s - 1, t_last)
        rs_step(1, s, only_main)
        opair[0, s - 2] = pair_product(0, s - 1)

    products(1, 3)
    both(2, 6, True)

    @pl.loop(3, 8)
    def _(s):
        products(1, s + 1)
        both(s)

    both(8, 7)
    rs_final(1)
    ag_arrive(0, 8, 8)
    opair[0, 7] = pair_product(0, 8)

    def finish_with(q, second):
        opair[1, q - 1] = scale[0:1] * (opair[0, q - 1] - scale[1:2] * second)
        a_copy(q).start()

    def finish(q):
        finish_with(q, opair[1, q - 1])

    @pl.loop(1, 5)
    def _(t):
        ag_arrive(1, t)
        opair[1, t - 1] = pair_product(1, t)

        @pl.when(t == 2)
        def _():
            zs_all().wait_recv()
            total = zstat[0]
            for o in range(1, NZ):
                total = total + zstat[o]
            tstat[j] = total
            for e in range(1, 8):
                ts_copy(e).start()

        @pl.when(t == 3)
        def _():
            ts_all().wait_recv()
            total = tstat[0]
            for o in range(1, 8):
                total = total + tstat[o]
            ystat[y] = total
            for e in (1, 2, 3):
                ys_copy(e).start()

        @pl.when(t == 4)
        def _():
            ys_all().wait_recv()
            total = (ystat[0] + ystat[1]) + (ystat[2] + ystat[3])
            hsic = jnp.sum(total[:, :128], keepdims=True)
            gram_sq = jnp.sum(total[:, 128:], keepdims=True)
            factor = -2.0 * TOKENS * DS / (jnp.sqrt(gram_sq) * tn_ref[0])
            scale[0:1] = jnp.broadcast_to(factor, (1, 128))
            scale[1:2] = jnp.broadcast_to(hsic / gram_sq, (1, 128))
            pl.loop(1, 5)(finish)

    ag_arrive(1, 5)
    finish_with(5, pair_product(1, 5))
    pl.loop(1, 5)(stage_b)
    ag_arrive(1, 6)
    finish_with(6, pair_product(1, 6))
    stage_b(5)
    ag_arrive(1, 7, 7)
    finish_with(7, pair_product(1, 7))
    stage_b(6)
    ag_arrive(1, 8, 8)
    finish_with(8, pair_product(1, 8))
    stage_b(7)

    def ring_sent(ph, send, recv):
        for k in range(KS):
            for d in (0, 1):
                sent = rbuf.at[ph, d, pl.ds(0, 8 if main(d, k) else 7), pl.ds(k * KR, KR)]
                rcopy(sent, sent, send.at[ph, d, k], recv.at[ph, d, 0, k], zdev[d]).wait_send()

    ring_sent(0, rs_send, rs_recv)
    ring_sent(1, rs_send, rs_recv)
    pl.loop(1, 6)(stage_f)
    stage_b(8)
    ring_sent(0, ag_send, ag_recv)
    ring_sent(1, ag_send, ag_recv)
    for d in (1, 2, 3):
        y_copy(d).wait_send()

        @pl.when((y + 4 - d) % 4 != x)
        def _():
            p_copy(d, x).wait_send()

    zs_all().wait_send()
    ts_all().wait_send()
    ys_all().wait_send()
    pl.loop(6, 9)(stage_f)
    rcopy(cx, cx, a_send, a_recv.at[0], sib).wait_send()
    for d in (1, 2, 3):
        rcopy(xrecv.at[d - 1], xrecv.at[d - 1], b_send.at[d - 1], b_recv.at[d - 1, 0], xdev[d - 1]).wait_send()


def body(student, teacher, teacher_norm):
    f32, bf16 = jnp.float32, jnp.bfloat16
    dma = pltpu.SemaphoreType.DMA
    return pl.pallas_call(
        kernel,
        out_shape=jax.ShapeDtypeStruct((OT, SC), f32),
        in_specs=[
            pl.BlockSpec(memory_space=pl.ANY),
            pl.BlockSpec(memory_space=pl.ANY),
            pl.BlockSpec(memory_space=pltpu.SMEM),
        ],
        out_specs=pl.BlockSpec(memory_space=pltpu.VMEM),
        scratch_shapes=[
            pltpu.VMEM((TOK, SC), f32),
            pltpu.VMEM((TOK, TC), f32),
            dma((2,)),
            pltpu.VMEM((SC, TOK), bf16),
            pltpu.VMEM((SC, TOK), bf16),
            pltpu.VMEM((2, TOK, TC), bf16),
            pltpu.VMEM((2, TOK, TC), bf16),
            pltpu.VMEM((3, 128, TC), f32),
            pltpu.VMEM((TOK, TC), f32),
            pltpu.VMEM((2, SC, TC), f32),
            pltpu.VMEM((2, 2, 8, CH, TC), f32),
            pltpu.VMEM((2, SC, TC), f32),
            pltpu.VMEM((2, NP, 4, 2, OT, PW), f32),
            pltpu.VMEM((NP, 4, OT, PW), f32),
            pltpu.VMEM((NP, 4, OT, PW), f32),
            pltpu.VMEM((3, NP, OT, PW), f32),
            pltpu.VMEM((NZ, 1, 256), f32),
            pltpu.VMEM((8, 1, 256), f32),
            pltpu.VMEM((4, 1, 256), f32),
            pltpu.VMEM((8, 128), f32),
            dma((2, 2, KS)),
            dma((2, 2, 8, KS)),
            dma((2, 2, KS)),
            dma((2, 2, 8, KS)),
            dma((3,)),
            dma((3,)),
            dma((3,)),
            dma((4,)),
            dma,
            dma,
            dma,
            dma,
            dma,
            dma,
            dma,
            dma((8,)),
            dma((3,)),
            dma((3, 8)),
        ],
        compiler_params=pltpu.CompilerParams(
            collective_id=0, has_side_effects=True
        ),
    )(student, teacher, teacher_norm)


def solution(mesh):
    return jax.shard_map(
        body,
        mesh=mesh,
        in_specs=(P("tok", "scol"), P("tok", "tcol"), P()),
        out_specs=P(("tok", "tcol"), "scol"),
        check_vma=False,
    )
```

```python
import functools

import jax
import jax.numpy as jnp
from jax import lax
from jax.experimental import pallas as pl
from jax.experimental.pallas import tpu as pltpu
from jax.sharding import PartitionSpec as P

DS = 4096
TOKENS = 8192
MESH = pl.DeviceIdType.MESH
NZ = 16
TOK = 512
SC = 1024
TC = 512
CH = SC // NZ
KS = 4
KR = CH // KS
PW = 2 * CH
NP = SC // PW
OT = TOK // 8


def split(value):
    high = value.astype(jnp.bfloat16)
    return high, (value - high.astype(jnp.float32)).astype(jnp.bfloat16)


def dot3(ah, al, bh, bl, dims):
    def one(a, b):
        return lax.dot_general(a, b, (dims, ((), ())), preferred_element_type=jnp.float32)

    return one(ah, bh) + (one(ah, bl) + one(al, bh))


def kernel(
    s_ref,
    t_ref,
    tn_ref,
    out_ref,
    sbuf,
    tbuf,
    load_sem,
    st_hi,
    st_lo,
    ab_hi,
    ab_lo,
    yq,
    pbuf,
    own,
    rbuf,
    full,
    opair,
    cx,
    qbuf,
    xrecv,
    zstat,
    tstat,
    ystat,
    scale,
    rs_send,
    rs_recv,
    ag_send,
    ag_recv,
    y_send,
    y_recv,
    p_send,
    p_recv,
    st_send,
    st_recv,
    ts_send,
    ts_recv,
    ys_send,
    ys_recv,
    a_send,
    a_recv,
    b_send,
    b_recv,
):
    z = lax.axis_index("tok")
    y = lax.axis_index("scol")
    j = lax.axis_index("tcol")
    x = j // 2
    c = j % 2
    zdev = ({"tok": (z + 1) % NZ}, {"tok": (z + NZ - 1) % NZ})
    ydev = [{"scol": (y + d) % 4} for d in (1, 2, 3)]
    xdev = [{"tcol": ((x + d) % 4) * 2 + c} for d in (1, 2, 3)]
    sib = {"tcol": 2 * x + 1 - c}
    tdev = [{"tcol": (j + e) % 8} for e in range(1, 8)]

    barrier = pltpu.get_barrier_semaphore()
    for dev in (*zdev, *ydev, *tdev):
        pl.semaphore_signal(barrier, inc=1, device_id=dev, device_id_type=MESH)

    def rcopy(src, dst, ssem, rsem, dev):
        return pltpu.make_async_remote_copy(
            src_ref=src, dst_ref=dst, send_sem=ssem, recv_sem=rsem, device_id=dev, device_id_type=MESH
        )

    def rows(o, k):
        return pl.ds(pl.multiple_of(o * CH + k * KR, KR), KR)

    def rs_first(ph, d, k):
        o = (z + 8) % NZ
        return rcopy(
            own.at[ph, rows(o, k)],
            rbuf.at[ph, d, 0, pl.ds(k * KR, KR)],
            rs_send.at[ph, d, k],
            rs_recv.at[ph, d, 0, k],
            zdev[d],
        )

    def rs_copy(ph, d, s, k):
        return rcopy(
            rbuf.at[ph, d, s - 2, pl.ds(k * KR, KR)],
            rbuf.at[ph, d, s - 1, pl.ds(k * KR, KR)],
            rs_send.at[ph, d, k],
            rs_recv.at[ph, d, s - 1, k],
            zdev[d],
        )

    def rs_wait(ph, d, s, k):
        rcopy(
            rbuf.at[ph, d, s - 1, pl.ds(k * KR, KR)],
            rbuf.at[ph, d, s - 1, pl.ds(k * KR, KR)],
            rs_send.at[ph, d, k],
            rs_recv.at[ph, d, s - 1, k],
            zdev[d],
        ).wait_recv()

    def main(d, k):
        return (k < KS // 2) if d == 0 else (k >= KS // 2)

    def rs_second(ph, d, k):
        o = (z + 7) % NZ if d == 0 else (z + 9) % NZ
        return rcopy(
            own.at[ph, rows(o, k)],
            rbuf.at[ph, d, 1, pl.ds(k * KR, KR)],
            rs_send.at[ph, d, k],
            rs_recv.at[ph, d, 1, k],
            zdev[d],
        )

    def rs_start(ph):
        for k in range(KS):
            rs_first(ph, 0 if k < KS // 2 else 1, k).start()
        if ph == 0:
            prepare(2)
        products(ph, 2)
        for k in range(KS):
            rs_second(ph, 1 if k < KS // 2 else 0, k).start()

    def rs_step(ph, s, only_main=False):
        offs = ((z + 9 - s) % NZ, (z + s + 7) % NZ)
        for k in range(KS):
            for d in (0, 1):
                if only_main and not main(d, k):
                    continue
                here = (ph, d, s - 2, pl.ds(k * KR, KR))
                mine = own[ph, rows(offs[d], k)]
                rs_wait(ph, d, s - 1, k)
                rbuf[here] = rbuf[here] + mine
                rs_copy(ph, d, s, k).start()

    def rs_final(ph):
        total = jnp.zeros((8, 128), jnp.float32)
        for k in range(KS):
            for d in (0, 1):
                rs_wait(ph, d, 8, k)
            at = pl.ds(k * KR, KR)
            value = own[ph, rows(z, k)] + (rbuf[ph, 0, 7, at] + rbuf[ph, 1, 7, at])
            full[ph, rows(z, k)] = value
            square = value * value
            for a in range(0, KR, 8):
                for b in range(0, TC, 128):
                    total = total + square[a : a + 8, b : b + 128]
            if k < KS - 1:
                for d in (0, 1):
                    ag_copy(ph, d, 1, k).start()
        zstat[z, :, ph * 128 : ph * 128 + 128] = jnp.sum(total, axis=0, keepdims=True)
        if ph == 1:
            for e in range(1, NZ):
                zs_copy(e).start()
        for d in (0, 1):
            ag_copy(ph, d, 1, KS - 1).start()

    def ag_copy(ph, d, t, k):
        o = (z + NZ + 1 - t) % NZ if d == 0 else (z + t - 1) % NZ
        return rcopy(
            full.at[ph, rows(o, k)],
            full.at[ph, rows(o, k)],
            ag_send.at[ph, d, k],
            ag_recv.at[ph, d, t - 1, k],
            zdev[d],
        )

    def ag_wait(ph, d, t, k):
        o = (z + NZ - t) % NZ if d == 0 else (z + t) % NZ
        rcopy(
            full.at[ph, rows(o, k)],
            full.at[ph, rows(o, k)],
            ag_send.at[ph, d, k],
            ag_recv.at[ph, d, t - 1, k],
            zdev[d],
        ).wait_recv()

    def ag_arrive(ph, t, last=6):
        for k in range(KS):
            for d in (0, 1):
                if last < 8 or main(d, k):
                    ag_wait(ph, d, t, k)
                if last < 7 or (last == 7 and main(d, k)):
                    ag_copy(ph, d, t + 1, k).start()

    def block_of(s):
        up = (z + s) % 2
        p = ((up * (z + 7 + s) + (1 - up) * (z + 9 - s)) % NZ) // 2
        return pl.ds(pl.multiple_of(p * PW, PW), PW)

    def prepare(s):
        at = block_of(s)
        sh, sl = split(sbuf[:, at].T)
        st_hi[at] = sh
        st_lo[at] = sl

    def products(ph, s):
        at = block_of(s)
        own[ph, at] = dot3(st_hi[at], st_lo[at], ab_hi[ph], ab_lo[ph], ((1,), (0,)))

    def pair_of(t):
        up = (z + t) % 2
        return ((up * (z + t - 1) + (1 - up) * (z + NZ - t)) % NZ) // 2

    def pair_product(ph, t):
        p = pair_of(t)
        wh, wl = split(full[ph, pl.ds(pl.multiple_of(p * PW, PW), PW)])

        def one(a, b):
            return lax.dot_general(a, b, (((1,), (1,)), ((), ())), preferred_element_type=jnp.float32)

        wide = one(ab_hi[ph], jnp.concatenate([wh, wl], axis=0))
        value = wide[:, :PW] + (wide[:, PW:] + one(ab_lo[ph], wh))
        return value.reshape(4, 2, OT, PW)

    def zs_copy(e):
        return rcopy(zstat.at[z], zstat.at[z], st_send, st_recv, {"tok": (z + e) % NZ})

    def zs_all():
        part = zstat.at[pl.ds(0, NZ - 1)]
        return rcopy(part, part, st_send, st_recv, zdev[0])

    def ts_copy(e):
        return rcopy(tstat.at[j], tstat.at[j], ts_send, ts_recv, tdev[e - 1])

    def ts_all():
        part = tstat.at[pl.ds(0, 7)]
        return rcopy(part, part, ts_send, ts_recv, tdev[0])

    def ys_copy(e):
        return rcopy(ystat.at[y], ystat.at[y], ys_send, ys_recv, ydev[e - 1])

    def ys_all():
        part = ystat.at[pl.ds(0, 3)]
        return rcopy(part, part, ys_send, ys_recv, ydev[0])

    def y_copy(d):
        return rcopy(
            sbuf.at[pl.ds(pl.multiple_of(x * 128, 128), 128), pl.ds(pl.multiple_of(c * TC, TC), TC)],
            yq.at[d - 1],
            y_send.at[d - 1],
            y_recv.at[d - 1],
            ydev[d - 1],
        )

    def p_copy(d, at):
        return rcopy(
            yq.at[d - 1],
            pbuf.at[pl.ds(pl.multiple_of(at * 128, 128), 128)],
            p_send.at[d - 1],
            p_recv.at[at],
            {"tcol": ((y + 4 - d) % 4) * 2 + c},
        )

    def forward(d):
        source = (y + 4 - d) % 4
        y_copy(d).wait_recv()

        @pl.when(source == x)
        def _():
            pbuf[pl.ds(pl.multiple_of(x * 128, 128), 128)] = yq[d - 1]

        @pl.when(source != x)
        def _():
            p_copy(d, x).start()

    def a_copy(q):
        return rcopy(opair.at[1, q - 1, :, 1 - c], cx.at[q - 1], a_send, a_recv.at[q - 1], sib)

    def b_copy(q, d):
        return rcopy(
            qbuf.at[q - 1, (x + d) % 4],
            xrecv.at[d - 1, q - 1],
            b_send.at[d - 1],
            b_recv.at[d - 1, q - 1],
            xdev[d - 1],
        )

    def stage_b(q):
        a_copy(q).wait_recv()
        qbuf[q - 1] = opair[1, q - 1, :, c] + cx[q - 1]
        for d in (1, 3, 2):
            b_copy(q, d).start()

    def stage_f(q):
        for d in (1, 2, 3):
            b_copy(q, d).wait_recv()
        value = (qbuf[q - 1, x] + xrecv[0, q - 1]) + (xrecv[1, q - 1] + xrecv[2, q - 1])
        p = pair_of(q)
        out_ref[:, pl.ds(pl.multiple_of(p * PW, PW), PW)] = value

    loads = [pltpu.make_async_copy(t_ref, tbuf, load_sem.at[0]), pltpu.make_async_copy(s_ref, sbuf, load_sem.at[1])]
    for load in loads:
        load.start()
    loads[0].wait()
    th, tl = split(tbuf[...])
    ab_hi[0] = th
    ab_lo[0] = tl
    loads[1].wait()
    prepare(1)
    products(0, 1)
    pl.semaphore_wait(barrier, 12)
    for d in (1, 3, 2):
        y_copy(d).start()

    rs_start(0)
    prepare(3)
    products(0, 3)
    rs_step(0, 2, True)

    @pl.loop(3, 9)
    def _(s):
        @pl.when(s < 8)
        def _():
            prepare(s + 1)
            products(0, s + 1)

        rs_step(0, s)

        @pl.when(s == 3)
        def _():
            forward(1)
            forward(3)

        @pl.when(s == 5)
        def _():
            forward(2)

    rs_final(0)

    @pl.when(x == y)
    def _():
        pbuf[...] = sbuf[:, pl.ds(pl.multiple_of(c * TC, TC), TC)]

    @pl.when(x != y)
    def _():
        for e in (1, 2, 3):
            p_copy(1, (x + e) % 4).wait_recv()

    gh, gl = split(pbuf[...])
    ab_hi[1] = gh
    ab_lo[1] = gl
    products(1, 1)
    rs_start(1)

    def both(s, t_last=6, only_main=False):
        ag_arrive(0, s - 1, t_last)
        rs_step(1, s, only_main)
        opair[0, s - 2] = pair_product(0, s - 1)

    products(1, 3)
    both(2, 6, True)

    @pl.loop(3, 8)
    def _(s):
        products(1, s + 1)
        both(s)

    both(8, 7)
    rs_final(1)
    ag_arrive(0, 8, 8)
    opair[0, 7] = pair_product(0, 8)

    def finish_with(q, second):
        opair[1, q - 1] = scale[0:1] * (opair[0, q - 1] - scale[1:2] * second)
        a_copy(q).start()

    def finish(q):
        finish_with(q, opair[1, q - 1])

    @pl.loop(1, 5)
    def _(t):
        ag_arrive(1, t)
        opair[1, t - 1] = pair_product(1, t)

        @pl.when(t == 2)
        def _():
            zs_all().wait_recv()
            total = zstat[0]
            for o in range(1, NZ):
                total = total + zstat[o]
            tstat[j] = total
            for e in range(1, 8):
                ts_copy(e).start()

        @pl.when(t == 3)
        def _():
            ts_all().wait_recv()
            total = tstat[0]
            for o in range(1, 8):
                total = total + tstat[o]
            ystat[y] = total
            for e in (1, 2, 3):
                ys_copy(e).start()

        @pl.when(t == 4)
        def _():
            ys_all().wait_recv()
            total = (ystat[0] + ystat[1]) + (ystat[2] + ystat[3])
            hsic = jnp.sum(total[:, :128], keepdims=True)
            gram_sq = jnp.sum(total[:, 128:], keepdims=True)
            factor = -2.0 * TOKENS * DS / (jnp.sqrt(gram_sq) * tn_ref[0])
            scale[0:1] = jnp.broadcast_to(factor, (1, 128))
            scale[1:2] = jnp.broadcast_to(hsic / gram_sq, (1, 128))
            pl.loop(1, 3)(finish)

    ag_arrive(1, 5)
    opair[1, 4] = pair_product(1, 5)
    pl.loop(3, 5)(finish)
    pl.loop(1, 3)(stage_b)
    ag_arrive(1, 6)
    finish_with(6, pair_product(1, 6))
    finish(5)
    pl.loop(3, 5)(stage_b)
    ag_arrive(1, 7, 7)
    finish_with(7, pair_product(1, 7))
    pl.loop(5, 7)(stage_b)
    ag_arrive(1, 8, 8)
    finish_with(8, pair_product(1, 8))
    stage_b(7)

    def ring_sent(ph, send, recv):
        for k in range(KS):
            for d in (0, 1):
                sent = rbuf.at[ph, d, pl.ds(0, 8 if main(d, k) else 7), pl.ds(k * KR, KR)]
                rcopy(sent, sent, send.at[ph, d, k], recv.at[ph, d, 0, k], zdev[d]).wait_send()

    ring_sent(0, rs_send, rs_recv)
    ring_sent(1, rs_send, rs_recv)
    pl.loop(1, 6)(stage_f)
    stage_b(8)
    ring_sent(0, ag_send, ag_recv)
    ring_sent(1, ag_send, ag_recv)
    for d in (1, 2, 3):
        y_copy(d).wait_send()

        @pl.when((y + 4 - d) % 4 != x)
        def _():
            p_copy(d, x).wait_send()

    zs_all().wait_send()
    ts_all().wait_send()
    ys_all().wait_send()
    pl.loop(6, 9)(stage_f)
    rcopy(cx, cx, a_send, a_recv.at[0], sib).wait_send()
    for d in (1, 2, 3):
        rcopy(xrecv.at[d - 1], xrecv.at[d - 1], b_send.at[d - 1], b_recv.at[d - 1, 0], xdev[d - 1]).wait_send()


def body(student, teacher, teacher_norm):
    f32, bf16 = jnp.float32, jnp.bfloat16
    dma = pltpu.SemaphoreType.DMA
    return pl.pallas_call(
        kernel,
        out_shape=jax.ShapeDtypeStruct((OT, SC), f32),
        in_specs=[
            pl.BlockSpec(memory_space=pltpu.HBM),
            pl.BlockSpec(memory_space=pltpu.HBM),
            pl.BlockSpec(memory_space=pltpu.SMEM),
        ],
        out_specs=pl.BlockSpec(memory_space=pltpu.VMEM),
        scratch_shapes=[
            pltpu.VMEM((TOK, SC), f32),
            pltpu.VMEM((TOK, TC), f32),
            dma((2,)),
            pltpu.VMEM((SC, TOK), bf16),
            pltpu.VMEM((SC, TOK), bf16),
            pltpu.VMEM((2, TOK, TC), bf16),
            pltpu.VMEM((2, TOK, TC), bf16),
            pltpu.VMEM((3, 128, TC), f32),
            pltpu.VMEM((TOK, TC), f32),
            pltpu.VMEM((2, SC, TC), f32),
            pltpu.VMEM((2, 2, 8, CH, TC), f32),
            pltpu.VMEM((2, SC, TC), f32),
            pltpu.VMEM((2, NP, 4, 2, OT, PW), f32),
            pltpu.VMEM((NP, 4, OT, PW), f32),
            pltpu.VMEM((NP, 4, OT, PW), f32),
            pltpu.VMEM((3, NP, OT, PW), f32),
            pltpu.VMEM((NZ, 1, 256), f32),
            pltpu.VMEM((8, 1, 256), f32),
            pltpu.VMEM((4, 1, 256), f32),
            pltpu.VMEM((8, 128), f32),
            dma((2, 2, KS)),
            dma((2, 2, 8, KS)),
            dma((2, 2, KS)),
            dma((2, 2, 8, KS)),
            dma((3,)),
            dma((3,)),
            dma((3,)),
            dma((4,)),
            dma,
            dma,
            dma,
            dma,
            dma,
            dma,
            dma,
            dma((8,)),
            dma((3,)),
            dma((3, 8)),
        ],
        compiler_params=pltpu.CompilerParams(
            collective_id=0, has_side_effects=True, vmem_limit_bytes=55_750_000
        ),
    )(student, teacher, teacher_norm)


def solution(mesh):
    return jax.shard_map(
        body,
        mesh=mesh,
        in_specs=(P("tok", "scol"), P("tok", "tcol"), P()),
        out_specs=P(("tok", "tcol"), "scol"),
        check_vma=False,
    )
```

```python
import functools

import jax
import jax.numpy as jnp
from jax import lax
from jax.experimental import pallas as pl
from jax.experimental.pallas import tpu as pltpu
from jax.sharding import PartitionSpec as P

DS = 4096
TOKENS = 8192
MESH = pl.DeviceIdType.MESH
NZ = 16
TOK = 512
SC = 1024
TC = 512
CH = SC // NZ
KS = 4
KR = CH // KS
PW = 2 * CH
NP = SC // PW
OT = TOK // 8


def split(value):
    high = value.astype(jnp.bfloat16)
    return high, (value - high.astype(jnp.float32)).astype(jnp.bfloat16)


def dot3(ah, al, bh, bl, dims):
    def one(a, b):
        return lax.dot_general(a, b, (dims, ((), ())), preferred_element_type=jnp.float32)

    return one(ah, bh) + (one(ah, bl) + one(al, bh))


def kernel(
    s_ref,
    t_ref,
    tn_ref,
    out_ref,
    sbuf,
    tbuf,
    load_sem,
    st_hi,
    st_lo,
    ab_hi,
    ab_lo,
    yq,
    pbuf,
    own,
    rbuf,
    full,
    opair,
    cx,
    qbuf,
    xrecv,
    zstat,
    tstat,
    ystat,
    scale,
    rs_send,
    rs_recv,
    ag_send,
    ag_recv,
    y_send,
    y_recv,
    p_send,
    p_recv,
    st_send,
    st_recv,
    ts_send,
    ts_recv,
    ys_send,
    ys_recv,
    a_send,
    a_recv,
    b_send,
    b_recv,
    last,
    e_send,
    e_recv,
):
    z = lax.axis_index("tok")
    y = lax.axis_index("scol")
    j = lax.axis_index("tcol")
    x = j // 2
    c = j % 2
    zdev = ({"tok": (z + 1) % NZ}, {"tok": (z + NZ - 1) % NZ})
    ydev = [{"scol": (y + d) % 4} for d in (1, 2, 3)]
    xdev = [{"tcol": ((x + d) % 4) * 2 + c} for d in (1, 2, 3)]
    sib = {"tcol": 2 * x + 1 - c}
    tdev = [{"tcol": (j + e) % 8} for e in range(1, 8)]

    barrier = pltpu.get_barrier_semaphore()
    for dev in (*zdev, *ydev, *tdev):
        pl.semaphore_signal(barrier, inc=1, device_id=dev, device_id_type=MESH)

    def rcopy(src, dst, ssem, rsem, dev):
        return pltpu.make_async_remote_copy(
            src_ref=src, dst_ref=dst, send_sem=ssem, recv_sem=rsem, device_id=dev, device_id_type=MESH
        )

    def rows(o, k):
        return pl.ds(pl.multiple_of(o * CH + k * KR, KR), KR)

    def rs_first(ph, d, k):
        o = (z + 8) % NZ
        return rcopy(
            own.at[ph, rows(o, k)],
            rbuf.at[ph, d, 0, pl.ds(k * KR, KR)],
            rs_send.at[ph, d, k],
            rs_recv.at[ph, d, 0, k],
            zdev[d],
        )

    def rs_copy(ph, d, s, k):
        return rcopy(
            rbuf.at[ph, d, s - 2, pl.ds(k * KR, KR)],
            rbuf.at[ph, d, s - 1, pl.ds(k * KR, KR)],
            rs_send.at[ph, d, k],
            rs_recv.at[ph, d, s - 1, k],
            zdev[d],
        )

    def rs_wait(ph, d, s, k):
        rcopy(
            rbuf.at[ph, d, s - 1, pl.ds(k * KR, KR)],
            rbuf.at[ph, d, s - 1, pl.ds(k * KR, KR)],
            rs_send.at[ph, d, k],
            rs_recv.at[ph, d, s - 1, k],
            zdev[d],
        ).wait_recv()

    def main(d, k):
        return (k < KS // 2) if d == 0 else (k >= KS // 2)

    def rs_second(ph, d, k):
        o = (z + 7) % NZ if d == 0 else (z + 9) % NZ
        return rcopy(
            own.at[ph, rows(o, k)],
            rbuf.at[ph, d, 1, pl.ds(k * KR, KR)],
            rs_send.at[ph, d, k],
            rs_recv.at[ph, d, 1, k],
            zdev[d],
        )

    def rs_start(ph):
        for k in range(KS):
            rs_first(ph, 0 if k < KS // 2 else 1, k).start()
        if ph == 0:
            prepare(2)
        products(ph, 2)
        for k in range(KS):
            rs_second(ph, 1 if k < KS // 2 else 0, k).start()

    def rs_step(ph, s, only_main=False):
        offs = ((z + 9 - s) % NZ, (z + s + 7) % NZ)
        for k in range(KS):
            for d in (0, 1):
                if only_main and not main(d, k):
                    continue
                here = (ph, d, s - 2, pl.ds(k * KR, KR))
                mine = own[ph, rows(offs[d], k)]
                rs_wait(ph, d, s - 1, k)
                rbuf[here] = rbuf[here] + mine
                rs_copy(ph, d, s, k).start()

    def rs_final(ph):
        total = jnp.zeros((8, 128), jnp.float32)
        for k in range(KS):
            for d in (0, 1):
                rs_wait(ph, d, 8, k)
            at = pl.ds(k * KR, KR)
            value = own[ph, rows(z, k)] + (rbuf[ph, 0, 7, at] + rbuf[ph, 1, 7, at])
            full[ph, rows(z, k)] = value
            square = value * value
            for a in range(0, KR, 8):
                for b in range(0, TC, 128):
                    total = total + square[a : a + 8, b : b + 128]
            if k < KS - 1:
                for d in (0, 1):
                    ag_copy(ph, d, 1, k).start()
        zstat[z, :, ph * 128 : ph * 128 + 128] = jnp.sum(total, axis=0, keepdims=True)
        for d in (0, 1):
            ag_copy(ph, d, 1, KS - 1).start()
        if ph == 1:
            for e in range(1, NZ):
                zs_copy(e).start()

    def ag_copy(ph, d, t, k):
        o = (z + NZ + 1 - t) % NZ if d == 0 else (z + t - 1) % NZ
        return rcopy(
            full.at[ph, rows(o, k)],
            full.at[ph, rows(o, k)],
            ag_send.at[ph, d, k],
            ag_recv.at[ph, d, t - 1, k],
            zdev[d],
        )

    def ag_wait(ph, d, t, k):
        o = (z + NZ - t) % NZ if d == 0 else (z + t) % NZ
        rcopy(
            full.at[ph, rows(o, k)],
            full.at[ph, rows(o, k)],
            ag_send.at[ph, d, k],
            ag_recv.at[ph, d, t - 1, k],
            zdev[d],
        ).wait_recv()

    def ag_arrive(ph, t, last=6):
        for k in range(KS):
            for d in (0, 1):
                if last < 8 or main(d, k):
                    ag_wait(ph, d, t, k)
                if last < 7 or (last == 7 and main(d, k)):
                    ag_copy(ph, d, t + 1, k).start()

    def block_of(s):
        up = (z + s) % 2
        p = ((up * (z + 7 + s) + (1 - up) * (z + 9 - s)) % NZ) // 2
        return pl.ds(pl.multiple_of(p * PW, PW), PW)

    def prepare(s):
        at = block_of(s)
        sh, sl = split(sbuf[:, at].T)
        st_hi[at] = sh
        st_lo[at] = sl

    def products(ph, s):
        at = block_of(s)
        own[ph, at] = dot3(st_hi[at], st_lo[at], ab_hi[ph], ab_lo[ph], ((1,), (0,)))

    def pair_of(t):
        up = (z + t) % 2
        return ((up * (z + t - 1) + (1 - up) * (z + NZ - t)) % NZ) // 2

    def pair_product(ph, t):
        p = pair_of(t)
        wh, wl = split(full[ph, pl.ds(pl.multiple_of(p * PW, PW), PW)])

        def one(a, b):
            return lax.dot_general(a, b, (((1,), (1,)), ((), ())), preferred_element_type=jnp.float32)

        wide = one(ab_hi[ph], jnp.concatenate([wh, wl], axis=0))
        value = wide[:, :PW] + (wide[:, PW:] + one(ab_lo[ph], wh))
        return value.reshape(4, 2, OT, PW)

    def zs_copy(e):
        return rcopy(zstat.at[z], zstat.at[z], st_send, st_recv, {"tok": (z + e) % NZ})

    def zs_all():
        part = zstat.at[pl.ds(0, NZ - 1)]
        return rcopy(part, part, st_send, st_recv, zdev[0])

    def ts_copy(e):
        return rcopy(tstat.at[j], tstat.at[j], ts_send, ts_recv, tdev[e - 1])

    def ts_all():
        part = tstat.at[pl.ds(0, 7)]
        return rcopy(part, part, ts_send, ts_recv, tdev[0])

    def ys_copy(e):
        return rcopy(ystat.at[y], ystat.at[y], ys_send, ys_recv, ydev[e - 1])

    def ys_all():
        part = ystat.at[pl.ds(0, 3)]
        return rcopy(part, part, ys_send, ys_recv, ydev[0])

    def y_copy(d):
        return rcopy(
            sbuf.at[pl.ds(pl.multiple_of(x * 128, 128), 128), pl.ds(pl.multiple_of(c * TC, TC), TC)],
            yq.at[d - 1],
            y_send.at[d - 1],
            y_recv.at[d - 1],
            ydev[d - 1],
        )

    def p_copy(d, at):
        return rcopy(
            yq.at[d - 1],
            pbuf.at[pl.ds(pl.multiple_of(at * 128, 128), 128)],
            p_send.at[d - 1],
            p_recv.at[at],
            {"tcol": ((y + 4 - d) % 4) * 2 + c},
        )

    def forward(d):
        source = (y + 4 - d) % 4
        y_copy(d).wait_recv()

        @pl.when(source == x)
        def _():
            pbuf[pl.ds(pl.multiple_of(x * 128, 128), 128)] = yq[d - 1]

        @pl.when(source != x)
        def _():
            p_copy(d, x).start()

    def a_copy(q):
        return rcopy(opair.at[1, q - 1, :, 1 - c], cx.at[q - 1], a_send, a_recv.at[q - 1], sib)

    def b_copy(q, d):
        return rcopy(
            qbuf.at[q - 1, (x + d) % 4],
            xrecv.at[d - 1, q - 1],
            b_send.at[d - 1],
            b_recv.at[d - 1, q - 1],
            xdev[d - 1],
        )

    def e_copy(e):
        o = (j + e) % 8
        return rcopy(opair.at[1, NP - 1, o // 2, o % 2], last.at[j], e_send, e_recv, tdev[e - 1])

    def e_all():
        part = last.at[pl.ds(0, 7)]
        return rcopy(part, part, e_send, e_recv, tdev[0])

    def stage_b(q):
        a_copy(q).wait_recv()
        qbuf[q - 1] = opair[1, q - 1, :, c] + cx[q - 1]
        for d in (1, 3, 2):
            b_copy(q, d).start()

    def stage_f(q):
        for d in (1, 2, 3):
            b_copy(q, d).wait_recv()
        value = (qbuf[q - 1, x] + xrecv[0, q - 1]) + (xrecv[1, q - 1] + xrecv[2, q - 1])
        p = pair_of(q)
        out_ref[:, pl.ds(pl.multiple_of(p * PW, PW), PW)] = value

    loads = [pltpu.make_async_copy(t_ref, tbuf, load_sem.at[0]), pltpu.make_async_copy(s_ref, sbuf, load_sem.at[1])]
    for load in loads:
        load.start()
    loads[0].wait()
    th, tl = split(tbuf[...])
    ab_hi[0] = th
    ab_lo[0] = tl
    loads[1].wait()
    prepare(1)
    products(0, 1)
    pl.semaphore_wait(barrier, 12)
    for d in (1, 3, 2):
        y_copy(d).start()

    rs_start(0)
    prepare(3)
    products(0, 3)
    rs_step(0, 2, True)

    @pl.loop(3, 9)
    def _(s):
        @pl.when(s < 8)
        def _():
            prepare(s + 1)
            products(0, s + 1)

        rs_step(0, s)

        @pl.when(s == 3)
        def _():
            forward(1)
            forward(3)

        @pl.when(s == 5)
        def _():
            forward(2)

    rs_final(0)

    @pl.when(x == y)
    def _():
        pbuf[...] = sbuf[:, pl.ds(pl.multiple_of(c * TC, TC), TC)]

    @pl.when(x != y)
    def _():
        for e in (1, 2, 3):
            p_copy(1, (x + e) % 4).wait_recv()

    gh, gl = split(pbuf[...])
    ab_hi[1] = gh
    ab_lo[1] = gl
    products(1, 1)
    rs_start(1)

    def both(s, t_last=6, only_main=False):
        ag_arrive(0, s - 1, t_last)
        rs_step(1, s, only_main)
        opair[0, s - 2] = pair_product(0, s - 1)

    products(1, 3)
    both(2, 6, True)

    @pl.loop(3, 8)
    def _(s):
        products(1, s + 1)
        both(s)

    both(8, 7)
    rs_final(1)
    ag_arrive(0, 8, 8)
    opair[0, 7] = pair_product(0, 8)

    def finish_with(q, second):
        opair[1, q - 1] = scale[0:1] * (opair[0, q - 1] - scale[1:2] * second)
        a_copy(q).start()

    def finish(q):
        finish_with(q, opair[1, q - 1])

    @pl.loop(1, 5)
    def _(t):
        ag_arrive(1, t)
        opair[1, t - 1] = pair_product(1, t)

        @pl.when(t == 2)
        def _():
            zs_all().wait_recv()
            total = zstat[0]
            for o in range(1, NZ):
                total = total + zstat[o]
            tstat[j] = total
            for e in range(1, 8):
                ts_copy(e).start()

        @pl.when(t == 3)
        def _():
            ts_all().wait_recv()
            total = tstat[0]
            for o in range(1, 8):
                total = total + tstat[o]
            ystat[y] = total
            for e in (1, 2, 3):
                ys_copy(e).start()

        @pl.when(t == 4)
        def _():
            ys_all().wait_recv()
            total = (ystat[0] + ystat[1]) + (ystat[2] + ystat[3])
            hsic = jnp.sum(total[:, :128], keepdims=True)
            gram_sq = jnp.sum(total[:, 128:], keepdims=True)
            factor = -2.0 * TOKENS * DS / (jnp.sqrt(gram_sq) * tn_ref[0])
            scale[0:1] = jnp.broadcast_to(factor, (1, 128))
            scale[1:2] = jnp.broadcast_to(hsic / gram_sq, (1, 128))
            pl.loop(1, 3)(finish)

    ag_arrive(1, 5)
    opair[1, 4] = pair_product(1, 5)
    pl.loop(3, 5)(finish)
    pl.loop(1, 3)(stage_b)
    ag_arrive(1, 6)
    finish_with(6, pair_product(1, 6))
    finish(5)
    pl.loop(3, 5)(stage_b)
    ag_arrive(1, 7, 7)
    finish_with(7, pair_product(1, 7))
    pl.loop(5, 7)(stage_b)
    ag_arrive(1, 8, 8)
    opair[1, 7] = scale[0:1] * (opair[0, 7] - scale[1:2] * pair_product(1, 8))
    for e in (2, 6, 3, 5, 4, 7, 1):
        e_copy(e).start()
    stage_b(7)

    def ring_sent(ph, send, recv):
        for k in range(KS):
            for d in (0, 1):
                sent = rbuf.at[ph, d, pl.ds(0, 8 if main(d, k) else 7), pl.ds(k * KR, KR)]
                rcopy(sent, sent, send.at[ph, d, k], recv.at[ph, d, 0, k], zdev[d]).wait_send()

    ring_sent(0, rs_send, rs_recv)
    ring_sent(1, rs_send, rs_recv)
    pl.loop(1, 6)(stage_f)
    ring_sent(0, ag_send, ag_recv)
    ring_sent(1, ag_send, ag_recv)
    for d in (1, 2, 3):
        y_copy(d).wait_send()

        @pl.when((y + 4 - d) % 4 != x)
        def _():
            p_copy(d, x).wait_send()

    zs_all().wait_send()
    ts_all().wait_send()
    ys_all().wait_send()
    pl.loop(6, 8)(stage_f)
    e_all().wait_recv()
    value = opair[1, 7, x, c]
    for e in range(1, 8):
        value = value + last[(j + e) % 8]
    out_ref[:, pl.ds(pl.multiple_of(pair_of(8) * PW, PW), PW)] = value
    e_all().wait_send()
    done = cx.at[pl.ds(0, 7)]
    rcopy(done, done, a_send, a_recv.at[0], sib).wait_send()
    for d in (1, 2, 3):
        done = xrecv.at[d - 1, pl.ds(0, 7)]
        rcopy(done, done, b_send.at[d - 1], b_recv.at[d - 1, 0], xdev[d - 1]).wait_send()


def body(student, teacher, teacher_norm):
    f32, bf16 = jnp.float32, jnp.bfloat16
    dma = pltpu.SemaphoreType.DMA
    return pl.pallas_call(
        kernel,
        out_shape=jax.ShapeDtypeStruct((OT, SC), f32),
        in_specs=[
            pl.BlockSpec(memory_space=pltpu.HBM),
            pl.BlockSpec(memory_space=pltpu.HBM),
            pl.BlockSpec(memory_space=pltpu.SMEM),
        ],
        out_specs=pl.BlockSpec(memory_space=pltpu.VMEM),
        scratch_shapes=[
            pltpu.VMEM((TOK, SC), f32),
            pltpu.VMEM((TOK, TC), f32),
            dma((2,)),
            pltpu.VMEM((SC, TOK), bf16),
            pltpu.VMEM((SC, TOK), bf16),
            pltpu.VMEM((2, TOK, TC), bf16),
            pltpu.VMEM((2, TOK, TC), bf16),
            pltpu.VMEM((3, 128, TC), f32),
            pltpu.VMEM((TOK, TC), f32),
            pltpu.VMEM((2, SC, TC), f32),
            pltpu.VMEM((2, 2, 8, CH, TC), f32),
            pltpu.VMEM((2, SC, TC), f32),
            pltpu.VMEM((2, NP, 4, 2, OT, PW), f32),
            pltpu.VMEM((NP, 4, OT, PW), f32),
            pltpu.VMEM((NP, 4, OT, PW), f32),
            pltpu.VMEM((3, NP, OT, PW), f32),
            pltpu.VMEM((NZ, 1, 256), f32),
            pltpu.VMEM((8, 1, 256), f32),
            pltpu.VMEM((4, 1, 256), f32),
            pltpu.VMEM((8, 128), f32),
            dma((2, 2, KS)),
            dma((2, 2, 8, KS)),
            dma((2, 2, KS)),
            dma((2, 2, 8, KS)),
            dma((3,)),
            dma((3,)),
            dma((3,)),
            dma((4,)),
            dma,
            dma,
            dma,
            dma,
            dma,
            dma,
            dma,
            dma((8,)),
            dma((3,)),
            dma((3, 8)),
            pltpu.VMEM((8, OT, PW), f32),
            dma,
            dma,
        ],
        compiler_params=pltpu.CompilerParams(
            collective_id=0, has_side_effects=True, vmem_limit_bytes=55_750_000
        ),
    )(student, teacher, teacher_norm)


def solution(mesh):
    return jax.shard_map(
        body,
        mesh=mesh,
        in_specs=(P("tok", "scol"), P("tok", "tcol"), P()),
        out_specs=P(("tok", "tcol"), "scol"),
        check_vma=False,
    )
```
